32 devices in a mesh: trc: 4 (over z), lat: 4 (over y, x), lon: 2 (over core).
Axes of the slice: x: 2, y: 2, z: 4, core: 2. Of those that a mesh axis runs over, the one named last changes fastest.
Arguments:
- tracers: float32 [8, 16, 128, 128], P('trc', 'lat', 'lon'), may hold values from -6 to 6
- land_mask: int32 [16, 128], P('lat', 'lon'), may hold values 0 or 1
- bottom_level: int32 [16, 128], P('lat', 'lon'), may hold values from 1 to 128
- bottom_part: float32 [16, 128], P('lat', 'lon'), may hold values from 0.05 to 1
- velocity: float32 [2, 2, 8, 32768], P(None, None, ('lat', 'lon'), 'trc'), may hold values from -0.45 to 0.45
- upwelling: float32 [2, 8, 32768], P(None, ('lat', 'lon'), 'trc'), may hold values from -0.3 to 0.3
- diffusivity: float32 [2, 8, 32768], P(None, ('lat', 'lon'), 'trc'), may hold values from 0.08 to 0.32
Outputs:
- tracers_out: float32 [8, 16, 128, 128], P('trc', 'lat', 'lon')
The draws below stay inside these ranges and needn't reach their ends.
All inputs are finite; a program needn't handle non-finite values. No bound on the sum of `land_mask` on one device may be relied on, other than what follows from the above.
Results may differ from the reference program's by a relative error of at most 0.0003.
Values sent between devices are 32-bit elements; how exact they have to be, the bound alone decides.
A program may use at most 64 MiB of HBM per device.

```python
import math
import jax
import jax.numpy as jnp
from jax import lax

ROWS = 4
COLS = 64
LEVELS = 128
STEPS = 2
NLAT = 16
NLON = 128
TRACERS = 8
BLOCKS = 8
CELLS_DEV = 32768
N_LAT = 4
N_LON = 2


def set_ends(drawn, own_key, least, high):
    spot = [jax.random.randint(jax.random.fold_in(own_key, axis), (), 0, length) for axis, length in enumerate(drawn.shape)]
    main_axis = drawn.shape.index(max(drawn.shape))
    neighbour = spot[:main_axis] + [(spot[main_axis] + 1) % drawn.shape[main_axis]] + spot[main_axis + 1:]
    return drawn.at[tuple(spot)].set(least).at[tuple(neighbour)].set(high)


def level_of(own_key, dims, shards, low, high):
    factor_of, own = 1.0, jax.random.fold_in(own_key, 6)
    for position, shards_of in shards:
        draws = jnp.exp(jax.random.uniform(jax.random.fold_in(own, position), (shards_of,), jnp.float32, low / len(shards), high / len(shards)))
        factor_of = factor_of * jnp.repeat(draws, dims[position] // shards_of).reshape([-1 if axis == position else 1 for axis in range(len(dims))])
    return factor_of


def noise(rng, shape, deviation, reach, split=(), dtype=jnp.bfloat16):
    values = deviation * jax.random.normal(rng, shape, jnp.float32)
    if split:
        values = values * level_of(rng, shape, split, -0.22, 0.18)
    return jnp.clip(values, -reach, reach).astype(dtype)


def setup_inputs(seed: int = 0) -> dict:
    key_list = jax.random.split(jax.random.key(seed), 8)
    tracers = noise(key_list[0], (TRACERS, NLAT, NLON, LEVELS), 1.0, 6.0, ((0, 4), (1, 4), (2, 2)), jnp.float32)
    land_mask = set_ends((jax.random.randint(key_list[1], (NLAT, NLON), 0, 8) < 7).astype(jnp.int32), jax.random.fold_in(key_list[1], 1), 0, 1)
    bottom_level = set_ends(jax.random.randint(key_list[2], (NLAT, NLON), 1, LEVELS + 1), jax.random.fold_in(key_list[2], 1), 1, LEVELS).astype(jnp.int32)
    bottom_part = jnp.clip(0.05 + 0.95 * jax.random.uniform(key_list[3], (NLAT, NLON), jnp.float32) ** level_of(key_list[3], (NLAT, NLON), ((0, 4), (1, 2)), -0.2, 0.2), 0.05, 1.0)
    velocity = jnp.clip(jax.random.uniform(key_list[4], (STEPS, 2, BLOCKS, CELLS_DEV), jnp.float32, -0.45, 0.45) * level_of(key_list[4], (STEPS, 2, BLOCKS, CELLS_DEV), ((2, 8), (3, 4)), -0.4, 0.0), -0.45, 0.45)
    upwelling = jnp.clip(jax.random.uniform(key_list[5], (STEPS, BLOCKS, CELLS_DEV), jnp.float32, -0.3, 0.3) * level_of(key_list[5], (STEPS, BLOCKS, CELLS_DEV), ((1, 8), (2, 4)), -0.4, 0.0), -0.3, 0.3)
    diffusivity = jnp.clip(jnp.exp(math.log(0.32) - 1.3862944 * jax.random.uniform(key_list[6], (STEPS, BLOCKS, CELLS_DEV), jnp.float32) ** level_of(key_list[6], (STEPS, BLOCKS, CELLS_DEV), ((1, 8), (2, 4)), -0.2, 0.2)), 0.08, 0.32)
    return {"tracers": tracers, "land_mask": land_mask, "bottom_level": bottom_level, "bottom_part": bottom_part, "velocity": velocity, "upwelling": upwelling, "diffusivity": diffusivity}


fraction_floor = 0.25


def minmod(first, second):
    return 0.5 * (jnp.sign(first) + jnp.sign(second)) * jnp.minimum(jnp.abs(first), jnp.abs(second))


def window(array, start, stop, offset):
    return lax.slice_in_dim(array, start, stop, axis=array.ndim + offset)


def face_divergence(field, speed, mixing, fraction, offset):
    extent = field.shape[field.ndim + offset]
    before = window(field, 0, extent - 3, offset)
    lower = window(field, 1, extent - 2, offset)
    upper = window(field, 2, extent - 1, offset)
    after = window(field, 3, extent, offset)
    face_speed = 0.5 * (window(speed, 1, extent - 2, offset) + window(speed, 2, extent - 1, offset))
    face_area = jnp.minimum(window(fraction, 1, extent - 2, offset), window(fraction, 2, extent - 1, offset))
    face_mixing = 0.5 * (window(mixing, 1, extent - 2, offset) + window(mixing, 2, extent - 1, offset))
    jump = upper - lower
    damping = 0.5 * (1.0 - jnp.abs(face_speed))
    from_lower = lower + damping * minmod(lower - before, jump)
    from_upper = upper - damping * minmod(jump, after - upper)
    face_value = jnp.where(face_speed >= 0.0, from_lower, from_upper)
    face_flux = face_area * (face_speed * face_value - face_mixing * jump)
    return window(face_flux, 1, extent - 3, offset) - window(face_flux, 0, extent - 4, offset)


def substep(field, fraction, eastward, northward, mixing, rising):
    across_rows = face_divergence(field, northward, mixing, fraction, -3)[..., 2:-2, :]
    across_cols = face_divergence(field, eastward, mixing, fraction, -2)[..., 2:-2, :, :]
    centre = field[..., 2:-2, 2:-2, :]
    wet_share = fraction[2:-2, 2:-2, :]
    top_area = jnp.minimum(wet_share[:, :, :-1], wet_share[:, :, 1:])
    lifting = rising[:, :, :-1]
    carried = jnp.where(lifting >= 0.0, centre[..., :-1], centre[..., 1:])
    vertical = top_area * lifting * carried
    closed = jnp.zeros(vertical.shape[:-1] + (1,), jnp.float32)
    across_levels = jnp.concatenate([vertical, closed], axis=-1) - jnp.concatenate([closed, vertical], axis=-1)
    return centre - (across_rows + across_cols + across_levels) / jnp.maximum(wet_share, fraction_floor)


def cell_fraction(land_mask, bottom_level, bottom_part, levels):
    level_index = lax.broadcasted_iota(jnp.int32, land_mask.shape + (levels,), 2)
    deepest = bottom_level[:, :, None].astype(jnp.int32) - 1
    full_cell = (level_index < deepest).astype(jnp.float32)
    last_cell = (level_index == deepest).astype(jnp.float32) * bottom_part[:, :, None]
    return land_mask.astype(jnp.float32)[:, :, None] * (full_cell + last_cell)


def unblock(array):
    leading = array.shape[:-2]
    array = array.reshape(leading + (N_LAT, N_LON, ROWS, COLS, LEVELS))
    array = jnp.swapaxes(array, -4, -3)
    return array.reshape(leading + (N_LAT * ROWS, N_LON * COLS, LEVELS))


def widen(array):
    return jnp.pad(array, ((2, 2), (2, 2), (0, 0)))


def reference(tracers, land_mask, bottom_level, bottom_part, velocity, upwelling, diffusivity):
    fraction = cell_fraction(land_mask, bottom_level, bottom_part, LEVELS)
    speeds = unblock(velocity)
    rises = unblock(upwelling)
    mixes = unblock(diffusivity)
    wide_frac = widen(fraction)

    def advance(field):
        for number in range(STEPS):
            field = substep(widen(field), wide_frac, widen(speeds[number, 0]), widen(speeds[number, 1]),
                            widen(mixes[number]), rises[number])
        return field

    return lax.map(advance, tracers)
```

```python
import functools

import jax
import jax.numpy as jnp
from jax import lax
from jax.experimental import pallas as pl
from jax.experimental.pallas import tpu as pltpu
from jax.sharding import PartitionSpec as P

STEPS = 2
MESH = pl.DeviceIdType.MESH


fraction_floor = 0.25


def with_halo(block, sides, width):
    for axis, dim in sides:
        count = lax.axis_size(axis)
        forward = [(i, i + 1) for i in range(count - 1)]
        backward = [(target, source) for source, target in forward]
        low = lax.ppermute(
            lax.slice_in_dim(block, block.shape[dim] - width, None, axis=dim), axis, forward
        )
        high = lax.ppermute(lax.slice_in_dim(block, 0, width, axis=dim), axis, backward)
        block = jnp.concatenate([low, block, high], axis=dim)
    return block


def minmod(first, second):
    return 0.5 * (jnp.sign(first) + jnp.sign(second)) * jnp.minimum(jnp.abs(first), jnp.abs(second))


def window(array, start, stop, offset):
    return lax.slice_in_dim(array, start, stop, axis=array.ndim + offset)


def face_divergence(field, speed, mixing, fraction, offset):
    extent = field.shape[field.ndim + offset]
    before = window(field, 0, extent - 3, offset)
    lower = window(field, 1, extent - 2, offset)
    upper = window(field, 2, extent - 1, offset)
    after = window(field, 3, extent, offset)
    face_speed = 0.5 * (window(speed, 1, extent - 2, offset) + window(speed, 2, extent - 1, offset))
    face_area = jnp.minimum(
        window(fraction, 1, extent - 2, offset), window(fraction, 2, extent - 1, offset)
    )
    face_mixing = 0.5 * (
        window(mixing, 1, extent - 2, offset) + window(mixing, 2, extent - 1, offset)
    )
    jump = upper - lower
    damping = 0.5 * (1.0 - jnp.abs(face_speed))
    from_lower = lower + damping * minmod(lower - before, jump)
    from_upper = upper - damping * minmod(jump, after - upper)
    face_value = jnp.where(face_speed >= 0.0, from_lower, from_upper)
    face_flux = face_area * (face_speed * face_value - face_mixing * jump)
    return window(face_flux, 1, extent - 3, offset) - window(face_flux, 0, extent - 4, offset)


def substep(field, fraction, eastward, northward, mixing, rising):
    across_rows = face_divergence(field, northward, mixing, fraction, -3)[..., 2:-2, :]
    across_cols = face_divergence(field, eastward, mixing, fraction, -2)[..., 2:-2, :, :]
    centre = field[..., 2:-2, 2:-2, :]
    wet_share = fraction[2:-2, 2:-2, :]
    top_area = jnp.minimum(wet_share[:, :, :-1], wet_share[:, :, 1:])
    lifting = rising[:, :, :-1]
    carried = jnp.where(lifting >= 0.0, centre[..., :-1], centre[..., 1:])
    vertical = top_area * lifting * carried
    closed = jnp.zeros(vertical.shape[:-1] + (1,), jnp.float32)
    across_levels = jnp.concatenate([vertical, closed], axis=-1) - jnp.concatenate(
        [closed, vertical], axis=-1
    )
    return centre - (across_rows + across_cols + across_levels) / jnp.maximum(
        wet_share, fraction_floor
    )


def cell_fraction(land_mask, bottom_level, bottom_part, levels):
    level_index = lax.broadcasted_iota(jnp.int32, land_mask.shape + (levels,), 2)
    deepest = bottom_level[:, :, None] - 1
    full_cell = (level_index < deepest).astype(jnp.float32)
    last_cell = (level_index == deepest).astype(jnp.float32) * bottom_part[:, :, None]
    return land_mask.astype(jnp.float32)[:, :, None] * (full_cell + last_cell)


def gathered_body(tracers, land_mask, bottom_level, bottom_part, velocity, upwelling, diffusivity):
    levels = tracers.shape[3]
    block_shape = (tracers.shape[1], tracers.shape[2], levels)
    fraction = cell_fraction(land_mask, bottom_level, bottom_part, levels)
    tracer_count = tracers.shape[0]
    moved = (
        lax.all_gather(velocity, "trc", axis=3, tiled=True),
        lax.all_gather(upwelling, "trc", axis=2, tiled=True),
        lax.all_gather(diffusivity, "trc", axis=2, tiled=True),
    )
    speeds = moved[0].reshape((STEPS, 2) + block_shape)
    rises = moved[1].reshape((STEPS,) + block_shape)
    mixes = moved[2].reshape((STEPS,) + block_shape)
    field = tracers
    wide_frac = fraction
    for number in range(STEPS):
        extras = [fraction[None]] if number == 0 else []
        stack = jnp.concatenate(
            [field] + extras + [jnp.stack([speeds[number, 0], speeds[number, 1], mixes[number]])],
            axis=0,
        )
        widened = with_halo(stack, (("lat", 1), ("lon", 2)), 2)
        if number == 0:
            wide_frac = widened[tracer_count]
        flows = widened[-3:]
        field = substep(
            widened[:tracer_count], wide_frac, flows[0], flows[1], flows[2], rises[number]
        )
    return field


U, K, V, W = range(4)
PAD = 8
CHUNK = 16


def limited_flux(before, lower, upper, after, east, scale, area_speed, area_mix):
    jump = upper - lower
    base = jnp.where(east, lower, upper)
    slope = jnp.where(east, lower - before, after - upper)
    limited = jnp.maximum(jnp.minimum(slope, jump), 0.0) + jnp.minimum(
        jnp.maximum(slope, jump), 0.0
    )
    return area_speed * (base + scale * limited) - area_mix * jump


def face_terms(speed_p, speed_q, mix_p, mix_q, frac_p, frac_q):
    speed = 0.5 * (speed_p + speed_q)
    area = jnp.minimum(frac_p, frac_q)
    east = speed >= 0.0
    damping = 0.5 * (1.0 - jnp.abs(speed))
    return east, jnp.where(east, damping, -damping), area * speed, area * (0.5 * (mix_p + mix_q))


def transport_kernel(
    counts, tr_hbm, vel_hbm, up_hbm, dif_hbm, mask_ref, level_ref, part_ref, out_ref,
    c0, c1, flow, frac, rflux, xflux,
    own_sem, in_sem, zs, zr, fs, cs, cr, fls, flr, frs, frr,
):
    n, n_lat, n_lon = counts
    tracer_count, rows, cols, levels = tr_hbm.shape
    t, la, lo = lax.axis_index("trc"), lax.axis_index("lat"), lax.axis_index("lon")
    inner = pl.ds(PAD, cols)
    left_halo, right_halo = pl.ds(0, PAD), pl.ds(PAD + cols, PAD)
    left_edge, right_edge = pl.ds(PAD, PAD), pl.ds(cols, PAD)

    sides = (
        (la > 0, {"lat": la - 1}),
        (la < n_lat - 1, {"lat": la + 1}),
        (lo > 0, {"lon": lo - 1}),
        (lo < n_lon - 1, {"lon": lo + 1}),
    )
    shifts = (1, -1, 2, -2)
    groups = tuple(((t + d >= 0) & (t + d < n), {"trc": t + d}) for d in shifts)

    barrier = pltpu.get_barrier_semaphore()
    for there, device in sides + groups:
        @pl.when(there)
        def _(device=device):
            pl.semaphore_signal(barrier, inc=1, device_id=device, device_id_type=MESH)
    total = 0
    for there, _ in sides + groups:
        total = total + jnp.where(there, 1, 0)
    pl.semaphore_wait(barrier, total)

    def source(s, f):
        return {
            U: lambda: vel_hbm.at[s, 0], V: lambda: vel_hbm.at[s, 1],
            K: lambda: dif_hbm.at[s], W: lambda: up_hbm.at[s],
        }[f]()

    def group_copy(s, f, i):
        return pltpu.make_async_remote_copy(
            src_ref=source(s, f), dst_ref=flow.at[s, f, 1 + t, inner],
            send_sem=zs.at[s, f, i], recv_sem=zr.at[s, f, t],
            device_id=groups[i][1], device_id_type=MESH,
        )

    def forward_copy(s, f, r, target):
        return pltpu.make_async_remote_copy(
            src_ref=flow.at[s, f, 1 + r, inner], dst_ref=flow.at[s, f, 1 + r, inner],
            send_sem=fs.at[s, f], recv_sem=zr.at[s, f, r],
            device_id={"trc": target}, device_id_type=MESH,
        )

    def own_copy(s, f):
        return pltpu.make_async_copy(
            source(s, f), flow.at[s, f, 1 + t, inner], own_sem.at[s, f]
        )

    def side_copy(src, dst, send, recv, i):
        return pltpu.make_async_remote_copy(
            src_ref=src, dst_ref=dst, send_sem=send.at[i], recv_sem=recv.at[i],
            device_id=sides[i][1], device_id_type=MESH,
        )

    def field_copy(s, i):
        dst = c0 if s == 0 else c1
        if s == 0:
            srcs = (
                tr_hbm.at[:, pl.ds(0, 2)], tr_hbm.at[:, pl.ds(rows - 2, 2)],
                tr_hbm.at[:, :, pl.ds(0, PAD)], tr_hbm.at[:, :, pl.ds(cols - PAD, PAD)],
            )
        else:
            srcs = (
                c1.at[:, pl.ds(2, 2), inner], c1.at[:, pl.ds(rows, 2), inner],
                c1.at[:, pl.ds(2, rows), left_edge], c1.at[:, pl.ds(2, rows), right_edge],
            )
        dsts = (
            dst.at[:, pl.ds(rows + 2, 2), inner], dst.at[:, pl.ds(0, 2), inner],
            dst.at[:, pl.ds(2, rows), right_halo], dst.at[:, pl.ds(2, rows), left_halo],
        )
        return side_copy(srcs[i], dsts[i], cs.at[s], cr.at[s], i)

    def frac_copy(i):
        body = pl.ds(1, rows)
        srcs = (frac.at[1, inner], frac.at[rows, inner],
                frac.at[body, left_edge], frac.at[body, right_edge])
        dsts = (frac.at[rows + 1, inner], frac.at[0, inner],
                frac.at[body, right_halo], frac.at[body, left_halo])
        return side_copy(srcs[i], dsts[i], frs, frr, i)

    def flow_copy(s, i):
        body = pl.ds(1, rows)
        kv, uk = pl.ds(K, 2), pl.ds(U, 2)
        srcs = (flow.at[s, kv, 1, inner], flow.at[s, kv, rows, inner],
                flow.at[s, uk, body, left_edge], flow.at[s, uk, body, right_edge])
        dsts = (flow.at[s, kv, rows + 1, inner], flow.at[s, kv, 0, inner],
                flow.at[s, uk, body, right_halo], flow.at[s, uk, body, left_halo])
        return side_copy(srcs[i], dsts[i], fls.at[s], flr.at[s], i)

    opposite = (1, 0, 3, 2)

    def on_sides(make, which, act):
        for i in which:
            @pl.when(sides[i][0])
            def _(i=i):
                getattr(make(i), act)()

    def receive(make, which):
        for i in which:
            @pl.when(sides[opposite[i]][0])
            def _(i=i):
                make(i).wait_recv()

    def start_group(s):
        for f in (K, V, U, W):
            for i in range(len(shifts)):
                @pl.when(groups[i][0])
                def _(f=f, i=i):
                    group_copy(s, f, i).start()

    start_group(0)
    own_field = pltpu.make_async_copy(tr_hbm, c0.at[:, pl.ds(2, rows), inner], in_sem)
    own_field.start()
    for f in (K, V, U, W):
        own_copy(0, f).start()
    on_sides(functools.partial(field_copy, 0), range(4), "start")
    start_group(1)
    for f in (K, V, U, W):
        own_copy(1, f).start()

    square = (cols, cols)
    eye = lax.broadcasted_iota(jnp.int32, square, 0) == lax.broadcasted_iota(jnp.int32, square, 1)
    level = lax.broadcasted_iota(jnp.int32, (cols, levels), 1).astype(jnp.float32)

    def upright(row):
        return jnp.sum(jnp.where(eye, jnp.broadcast_to(row, square), 0.0), axis=1, keepdims=True)

    for r in range(rows):
        wet = mask_ref[r:r + 1, :].astype(jnp.float32)
        deepest = upright(level_ref[r:r + 1, :].astype(jnp.float32) - 1.0)
        share = upright(wet * part_ref[r:r + 1, :])
        wet = upright(wet)
        frac[1 + r, inner, :] = jnp.where(
            level < deepest, wet, jnp.where(level == deepest, share, 0.0)
        )
    on_sides(frac_copy, range(4), "start")

    @pl.when(la == 0)
    def _():
        for field in (c0, c1):
            field[:, 0:2] = jnp.zeros((tracer_count, 2) + field.shape[2:], jnp.float32)
        frac[0] = jnp.zeros(frac.shape[1:], jnp.float32)
        flow[:, :, 0] = jnp.zeros((STEPS, 4) + flow.shape[3:], jnp.float32)

    @pl.when(la == n_lat - 1)
    def _():
        for field in (c0, c1):
            field[:, rows + 2:] = jnp.zeros((tracer_count, 2) + field.shape[2:], jnp.float32)
        frac[rows + 1] = jnp.zeros(frac.shape[1:], jnp.float32)
        flow[:, :, rows + 1] = jnp.zeros((STEPS, 4) + flow.shape[3:], jnp.float32)

    for at_edge, strip in ((lo == 0, left_halo), (lo == n_lon - 1, right_halo)):
        @pl.when(at_edge)
        def _(strip=strip):
            for field in (c0, c1):
                field[:, 2:2 + rows, strip] = jnp.zeros(
                    (tracer_count, rows, PAD, levels), jnp.float32)
            frac[1:1 + rows, strip] = jnp.zeros((rows, PAD, levels), jnp.float32)
            flow[:, :, 1:1 + rows, strip] = jnp.zeros((STEPS, 4, rows, PAD, levels), jnp.float32)

    own_field.wait()
    receive(frac_copy, range(4))

    def arrive(s, f, r):
        @pl.when(t == r)
        def _():
            own_copy(s, f).wait()

        @pl.when(t != r)
        def _():
            forward_copy(s, f, r, t).wait_recv()

    def collect(s):
        for f in (K, V, U, W):
            arrive(s, f, 0)

            @pl.when(t == n - 2)
            def _(f=f):
                forward_copy(s, f, 0, n - 1).start()
            arrive(s, f, n - 1)

            @pl.when(t == 1)
            def _(f=f):
                forward_copy(s, f, n - 1, 0).start()
            if f == V:
                on_sides(functools.partial(flow_copy, s), (0, 1), "start")
        for f in (K, V, U, W):
            for r in range(1, n - 1):
                arrive(s, f, r)
        on_sides(functools.partial(flow_copy, s), (2, 3), "start")
        receive(functools.partial(field_copy, s), range(4))
        receive(functools.partial(flow_copy, s), range(4))

    last_level = lax.broadcasted_iota(jnp.int32, (CHUNK, levels), 1) == levels - 1

    def advance(s, src, write):
        @pl.loop(0, rows + 1)
        def _(i):
            for c in range(0, cols, CHUNK):
                at = pl.ds(PAD + c, CHUNK)
                terms = face_terms(
                    flow[s, V, i, at], flow[s, V, i + 1, at],
                    flow[s, K, i, at], flow[s, K, i + 1, at], frac[i, at], frac[i + 1, at],
                )
                for a in range(tracer_count):
                    rflux[a, i, pl.ds(c, CHUNK)] = limited_flux(
                        src[a, i, at], src[a, i + 1, at], src[a, i + 2, at], src[a, i + 3, at],
                        *terms,
                    )

        @pl.loop(0, rows)
        def _(r):
            for c, size in [(c, CHUNK) for c in range(0, cols, CHUNK)] + [(cols - 7, 8)]:
                p, q = pl.ds(PAD + c - 1, size), pl.ds(PAD + c, size)
                terms = face_terms(
                    flow[s, U, r + 1, p], flow[s, U, r + 1, q],
                    flow[s, K, r + 1, p], flow[s, K, r + 1, q], frac[r + 1, p], frac[r + 1, q],
                )
                for a in range(tracer_count):
                    xflux[a, pl.ds(c, size)] = limited_flux(
                        src[a, r + 2, pl.ds(PAD + c - 2, size)], src[a, r + 2, p],
                        src[a, r + 2, q], src[a, r + 2, pl.ds(PAD + c + 1, size)], *terms,
                    )
            for c in range(0, cols, CHUNK):
                at = pl.ds(PAD + c, CHUNK)
                share = frac[r + 1, at]
                rise = flow[s, W, r + 1, at]
                area = jnp.where(
                    last_level, 0.0, jnp.minimum(share, pltpu.roll(share, levels - 1, 1))
                )
                lifted = area * rise
                upward = rise >= 0.0
                inverse = 1.0 / jnp.maximum(share, fraction_floor)
                for a in range(tracer_count):
                    centre = src[a, r + 2, at]
                    vertical = lifted * jnp.where(
                        upward, centre, pltpu.roll(centre, levels - 1, 1)
                    )
                    net = (
                        (rflux[a, r + 1, pl.ds(c, CHUNK)] - rflux[a, r, pl.ds(c, CHUNK)])
                        + (xflux[a, pl.ds(c + 1, CHUNK)] - xflux[a, pl.ds(c, CHUNK)])
                        + (vertical - pltpu.roll(vertical, 1, 1))
                    )
                    write(a, r, c, centre - net * inverse)

    def write_middle(a, r, c, value):
        c1[a, r + 2, pl.ds(PAD + c, CHUNK)] = value

    def write_out(a, r, c, value):
        out_ref[a, r, pl.ds(c, CHUNK)] = value

    collect(0)
    advance(0, c0, write_middle)
    on_sides(functools.partial(field_copy, 1), range(4), "start")
    collect(1)
    advance(1, c1, write_out)

    for s in range(STEPS):
        for f in range(4):
            for i in range(len(shifts)):
                @pl.when(groups[i][0])
                def _(s=s, f=f, i=i):
                    group_copy(s, f, i).wait_send()

            @pl.when((t == 1) | (t == n - 2))
            def _(s=s, f=f):
                forward_copy(s, f, 0, t).wait_send()
        on_sides(functools.partial(field_copy, s), range(4), "wait_send")
        on_sides(functools.partial(flow_copy, s), range(4), "wait_send")
    on_sides(frac_copy, range(4), "wait_send")


def fused_body(counts, tracers, land_mask, bottom_level, bottom_part, velocity, upwelling,
               diffusivity):
    tracer_count, rows, cols, levels = tracers.shape
    wide = cols + 2 * PAD
    row = (cols, levels)
    dma = pltpu.SemaphoreType.DMA
    hbm, vmem = pl.BlockSpec(memory_space=pl.ANY), pl.BlockSpec(memory_space=pltpu.VMEM)
    return pl.pallas_call(
        functools.partial(transport_kernel, counts),
        out_shape=jax.ShapeDtypeStruct(tracers.shape, jnp.float32),
        in_specs=[hbm] * 4 + [vmem] * 3,
        out_specs=vmem,
        scratch_shapes=[
            pltpu.VMEM((tracer_count, rows + 4, wide, levels), jnp.float32),
            pltpu.VMEM((tracer_count, rows + 4, wide, levels), jnp.float32),
            pltpu.VMEM((STEPS, 4, rows + 2, wide, levels), jnp.float32),
            pltpu.VMEM((rows + 2, wide, levels), jnp.float32),
            pltpu.VMEM((tracer_count, rows + 1, cols, levels), jnp.float32),
            pltpu.VMEM((tracer_count, cols + 8, levels), jnp.float32),
            dma((STEPS, 4)), dma,
            dma((STEPS, 4, 4)), dma((STEPS, 4, counts[0])), dma((STEPS, 4)),
            dma((STEPS, 4)), dma((STEPS, 4)),
            dma((STEPS, 4)), dma((STEPS, 4)),
            dma((4,)), dma((4,)),
        ],
        compiler_params=pltpu.CompilerParams(
            collective_id=0, has_side_effects=True, vmem_limit_bytes=32 * 1024 * 1024
        ),
    )(
        tracers,
        velocity.reshape((STEPS, 2) + row),
        upwelling.reshape((STEPS,) + row),
        diffusivity.reshape((STEPS,) + row),
        land_mask, bottom_level, bottom_part,
    )


def solution(mesh):
    placed = (
        P("trc", "lat", "lon", None),
        P("lat", "lon"),
        P("lat", "lon"),
        P("lat", "lon"),
        P(None, None, ("lat", "lon"), "trc"),
        P(None, ("lat", "lon"), "trc"),
        P(None, ("lat", "lon"), "trc"),
    )
    counts = tuple(mesh.shape[axis] for axis in ("trc", "lat", "lon"))

    def body(*arrays):
        tracers, velocity = arrays[0], arrays[4]
        one_row = velocity.shape[3] == tracers.shape[2] * tracers.shape[3]
        if counts[0] == 4 and tracers.shape[1] == 4 and one_row:
            return fused_body(counts, *arrays)
        return gathered_body(*arrays)

    return jax.shard_map(
        body, mesh=mesh, in_specs=placed, out_specs=P("trc", "lat", "lon", None), check_vma=False
    )
```

```python
import functools

import jax
import jax.numpy as jnp
from jax import lax
from jax.experimental import pallas as pl
from jax.experimental.pallas import tpu as pltpu
from jax.sharding import PartitionSpec as P

STEPS = 2
MESH = pl.DeviceIdType.MESH


fraction_floor = 0.25


def with_halo(block, sides, width):
    for axis, dim in sides:
        count = lax.axis_size(axis)
        forward = [(i, i + 1) for i in range(count - 1)]
        backward = [(target, source) for source, target in forward]
        low = lax.ppermute(
            lax.slice_in_dim(block, block.shape[dim] - width, None, axis=dim), axis, forward
        )
        high = lax.ppermute(lax.slice_in_dim(block, 0, width, axis=dim), axis, backward)
        block = jnp.concatenate([low, block, high], axis=dim)
    return block


def minmod(first, second):
    return 0.5 * (jnp.sign(first) + jnp.sign(second)) * jnp.minimum(jnp.abs(first), jnp.abs(second))


def window(array, start, stop, offset):
    return lax.slice_in_dim(array, start, stop, axis=array.ndim + offset)


def face_divergence(field, speed, mixing, fraction, offset):
    extent = field.shape[field.ndim + offset]
    before = window(field, 0, extent - 3, offset)
    lower = window(field, 1, extent - 2, offset)
    upper = window(field, 2, extent - 1, offset)
    after = window(field, 3, extent, offset)
    face_speed = 0.5 * (window(speed, 1, extent - 2, offset) + window(speed, 2, extent - 1, offset))
    face_area = jnp.minimum(
        window(fraction, 1, extent - 2, offset), window(fraction, 2, extent - 1, offset)
    )
    face_mixing = 0.5 * (
        window(mixing, 1, extent - 2, offset) + window(mixing, 2, extent - 1, offset)
    )
    jump = upper - lower
    damping = 0.5 * (1.0 - jnp.abs(face_speed))
    from_lower = lower + damping * minmod(lower - before, jump)
    from_upper = upper - damping * minmod(jump, after - upper)
    face_value = jnp.where(face_speed >= 0.0, from_lower, from_upper)
    face_flux = face_area * (face_speed * face_value - face_mixing * jump)
    return window(face_flux, 1, extent - 3, offset) - window(face_flux, 0, extent - 4, offset)


def substep(field, fraction, eastward, northward, mixing, rising):
    across_rows = face_divergence(field, northward, mixing, fraction, -3)[..., 2:-2, :]
    across_cols = face_divergence(field, eastward, mixing, fraction, -2)[..., 2:-2, :, :]
    centre = field[..., 2:-2, 2:-2, :]
    wet_share = fraction[2:-2, 2:-2, :]
    top_area = jnp.minimum(wet_share[:, :, :-1], wet_share[:, :, 1:])
    lifting = rising[:, :, :-1]
    carried = jnp.where(lifting >= 0.0, centre[..., :-1], centre[..., 1:])
    vertical = top_area * lifting * carried
    closed = jnp.zeros(vertical.shape[:-1] + (1,), jnp.float32)
    across_levels = jnp.concatenate([vertical, closed], axis=-1) - jnp.concatenate(
        [closed, vertical], axis=-1
    )
    return centre - (across_rows + across_cols + across_levels) / jnp.maximum(
        wet_share, fraction_floor
    )


def cell_fraction(land_mask, bottom_level, bottom_part, levels):
    level_index = lax.broadcasted_iota(jnp.int32, land_mask.shape + (levels,), 2)
    deepest = bottom_level[:, :, None] - 1
    full_cell = (level_index < deepest).astype(jnp.float32)
    last_cell = (level_index == deepest).astype(jnp.float32) * bottom_part[:, :, None]
    return land_mask.astype(jnp.float32)[:, :, None] * (full_cell + last_cell)


def gathered_body(tracers, land_mask, bottom_level, bottom_part, velocity, upwelling, diffusivity):
    levels = tracers.shape[3]
    block_shape = (tracers.shape[1], tracers.shape[2], levels)
    fraction = cell_fraction(land_mask, bottom_level, bottom_part, levels)
    tracer_count = tracers.shape[0]
    moved = (
        lax.all_gather(velocity, "trc", axis=3, tiled=True),
        lax.all_gather(upwelling, "trc", axis=2, tiled=True),
        lax.all_gather(diffusivity, "trc", axis=2, tiled=True),
    )
    speeds = moved[0].reshape((STEPS, 2) + block_shape)
    rises = moved[1].reshape((STEPS,) + block_shape)
    mixes = moved[2].reshape((STEPS,) + block_shape)
    field = tracers
    wide_frac = fraction
    for number in range(STEPS):
        extras = [fraction[None]] if number == 0 else []
        stack = jnp.concatenate(
            [field] + extras + [jnp.stack([speeds[number, 0], speeds[number, 1], mixes[number]])],
            axis=0,
        )
        widened = with_halo(stack, (("lat", 1), ("lon", 2)), 2)
        if number == 0:
            wide_frac = widened[tracer_count]
        flows = widened[-3:]
        field = substep(
            widened[:tracer_count], wide_frac, flows[0], flows[1], flows[2], rises[number]
        )
    return field


U, K, V, W = range(4)
PAD = 8
CHUNK = 16


def limited_flux(before, lower, upper, after, east, scale, area_speed, area_mix):
    jump = upper - lower
    base = jnp.where(east, lower, upper)
    slope = jnp.where(east, lower - before, after - upper)
    limited = jnp.maximum(jnp.minimum(slope, jump), 0.0) + jnp.minimum(
        jnp.maximum(slope, jump), 0.0
    )
    return area_speed * (base + scale * limited) - area_mix * jump


def face_terms(speed_p, speed_q, mix_p, mix_q, frac_p, frac_q):
    speed = 0.5 * (speed_p + speed_q)
    area = jnp.minimum(frac_p, frac_q)
    east = speed >= 0.0
    damping = 0.5 * (1.0 - jnp.abs(speed))
    return east, jnp.where(east, damping, -damping), area * speed, area * (0.5 * (mix_p + mix_q))


def transport_kernel(
    counts, tr_hbm, vel_hbm, up_hbm, dif_hbm, mask_hbm, level_hbm, part_hbm, out_ref,
    c0, c1, flow, frac, rflux, xflux, mask_ref, level_ref, part_ref,
    own_sem, in_sem, column_sem, zs, zr, fs, cs, cr, fls, flr, frs, frr,
):
    n, n_lat, n_lon = counts
    tracer_count, rows, cols, levels = tr_hbm.shape
    t, la, lo = lax.axis_index("trc"), lax.axis_index("lat"), lax.axis_index("lon")
    inner = pl.ds(PAD, cols)
    left_halo, right_halo = pl.ds(0, PAD), pl.ds(PAD + cols, PAD)
    left_edge, right_edge = pl.ds(PAD, PAD), pl.ds(cols, PAD)

    sides = (
        (la > 0, {"lat": la - 1}),
        (la < n_lat - 1, {"lat": la + 1}),
        (lo > 0, {"lon": lo - 1}),
        (lo < n_lon - 1, {"lon": lo + 1}),
    )
    shifts = (2, -2, 1, -1)
    groups = (
        (t < n - 2, {"trc": t + 2}), (t >= 2, {"trc": t - 2}),
        (t < n - 1, {"trc": t + 1}), (t > 0, {"trc": t - 1}),
    )
    relays = ((t == n - 2, n - 1, (0,)), (t == 1, 0, (n - 1,)))

    columns = [
        pltpu.make_async_copy(src, dst, column_sem.at[i])
        for i, (src, dst) in enumerate(
            ((mask_hbm, mask_ref), (level_hbm, level_ref), (part_hbm, part_ref)))
    ]
    for copy in columns:
        copy.start()
    barrier = pltpu.get_barrier_semaphore()
    partners = sides + groups
    for there, device in partners:
        @pl.when(there)
        def _(device=device):
            pl.semaphore_signal(barrier, inc=1, device_id=device, device_id_type=MESH)
    total = 0
    for there, _ in partners:
        total = total + jnp.where(there, 1, 0)
    pl.semaphore_wait(barrier, total)

    def source(s, f):
        return {
            U: lambda: vel_hbm.at[s, 0], V: lambda: vel_hbm.at[s, 1],
            K: lambda: dif_hbm.at[s], W: lambda: up_hbm.at[s],
        }[f]()

    def group_copy(s, f, i):
        return pltpu.make_async_remote_copy(
            src_ref=source(s, f), dst_ref=flow.at[s, f, 1 + t, inner],
            send_sem=zs.at[s, f, i], recv_sem=zr.at[s, f, t],
            device_id=groups[i][1], device_id_type=MESH,
        )

    def forward_copy(s, f, r, target, slot=0):
        return pltpu.make_async_remote_copy(
            src_ref=flow.at[s, f, 1 + r, inner], dst_ref=flow.at[s, f, 1 + r, inner],
            send_sem=fs.at[s, f, slot], recv_sem=zr.at[s, f, r],
            device_id={"trc": target}, device_id_type=MESH,
        )

    def own_copy(s, f):
        return pltpu.make_async_copy(
            source(s, f), flow.at[s, f, 1 + t, inner], own_sem.at[s, f]
        )

    def side_copy(src, dst, send, recv, i):
        return pltpu.make_async_remote_copy(
            src_ref=src, dst_ref=dst, send_sem=send.at[i], recv_sem=recv.at[i],
            device_id=sides[i][1], device_id_type=MESH,
        )

    def field_copy(s, i):
        dst = c0 if s == 0 else c1
        if s == 0:
            srcs = (
                tr_hbm.at[:, pl.ds(0, 2)], tr_hbm.at[:, pl.ds(rows - 2, 2)],
                tr_hbm.at[:, :, pl.ds(0, PAD)], tr_hbm.at[:, :, pl.ds(cols - PAD, PAD)],
            )
        else:
            srcs = (
                c1.at[:, pl.ds(2, 2), inner], c1.at[:, pl.ds(rows, 2), inner],
                c1.at[:, pl.ds(2, rows), left_edge], c1.at[:, pl.ds(2, rows), right_edge],
            )
        dsts = (
            dst.at[:, pl.ds(rows + 2, 2), inner], dst.at[:, pl.ds(0, 2), inner],
            dst.at[:, pl.ds(2, rows), right_halo], dst.at[:, pl.ds(2, rows), left_halo],
        )
        return side_copy(srcs[i], dsts[i], cs.at[s], cr.at[s], i)

    def frac_copy(i):
        body = pl.ds(1, rows)
        srcs = (frac.at[1, inner], frac.at[rows, inner],
                frac.at[body, left_edge], frac.at[body, right_edge])
        dsts = (frac.at[rows + 1, inner], frac.at[0, inner],
                frac.at[body, right_halo], frac.at[body, left_halo])
        return side_copy(srcs[i], dsts[i], frs, frr, i)

    def flow_copy(s, i):
        body = pl.ds(1, rows)
        kv, uk = pl.ds(K, 2), pl.ds(U, 2)
        srcs = (flow.at[s, kv, 1, inner], flow.at[s, kv, rows, inner],
                flow.at[s, uk, body, left_edge], flow.at[s, uk, body, right_edge])
        dsts = (flow.at[s, kv, rows + 1, inner], flow.at[s, kv, 0, inner],
                flow.at[s, uk, body, right_halo], flow.at[s, uk, body, left_halo])
        return side_copy(srcs[i], dsts[i], fls.at[s], flr.at[s], i)

    opposite = (1, 0, 3, 2)

    def on_sides(make, which, act):
        for i in which:
            @pl.when(sides[i][0])
            def _(i=i):
                getattr(make(i), act)()

    def receive(make, which):
        for i in which:
            @pl.when(sides[opposite[i]][0])
            def _(i=i):
                make(i).wait_recv()

    def start_group(s):
        for f in (K, V, U, W):
            for i in range(len(shifts)):
                @pl.when(groups[i][0])
                def _(f=f, i=i):
                    group_copy(s, f, i).start()

    start_group(0)
    own_field = pltpu.make_async_copy(tr_hbm, c0.at[:, pl.ds(2, rows), inner], in_sem)
    own_field.start()
    for f in (K, V, U, W):
        own_copy(0, f).start()
    on_sides(functools.partial(field_copy, 0), range(4), "start")

    start_group(1)
    for f in (K, V, U, W):
        own_copy(1, f).start()

    square = (cols, cols)
    eye = lax.broadcasted_iota(jnp.int32, square, 0) == lax.broadcasted_iota(jnp.int32, square, 1)
    level = lax.broadcasted_iota(jnp.int32, (cols, levels), 1).astype(jnp.float32)

    def upright(row):
        return jnp.sum(jnp.where(eye, jnp.broadcast_to(row, square), 0.0), axis=1, keepdims=True)

    for copy in columns:
        copy.wait()
    for r in range(rows):
        wet = mask_ref[r:r + 1, :].astype(jnp.float32)
        deepest = upright(level_ref[r:r + 1, :].astype(jnp.float32) - 1.0)
        share = upright(wet * part_ref[r:r + 1, :])
        wet = upright(wet)
        frac[1 + r, inner, :] = jnp.where(
            level < deepest, wet, jnp.where(level == deepest, share, 0.0)
        )
    on_sides(frac_copy, range(4), "start")

    @pl.when(la == 0)
    def _():
        for field in (c0, c1):
            field[:, 0:2] = jnp.zeros((tracer_count, 2) + field.shape[2:], jnp.float32)
        frac[0] = jnp.zeros(frac.shape[1:], jnp.float32)
        flow[:, :, 0] = jnp.zeros((STEPS, 4) + flow.shape[3:], jnp.float32)

    @pl.when(la == n_lat - 1)
    def _():
        for field in (c0, c1):
            field[:, rows + 2:] = jnp.zeros((tracer_count, 2) + field.shape[2:], jnp.float32)
        frac[rows + 1] = jnp.zeros(frac.shape[1:], jnp.float32)
        flow[:, :, rows + 1] = jnp.zeros((STEPS, 4) + flow.shape[3:], jnp.float32)

    for at_edge, strip in ((lo == 0, left_halo), (lo == n_lon - 1, right_halo)):
        @pl.when(at_edge)
        def _(strip=strip):
            for field in (c0, c1):
                field[:, 2:2 + rows, strip] = jnp.zeros(
                    (tracer_count, rows, PAD, levels), jnp.float32)
            frac[1:1 + rows, strip] = jnp.zeros((rows, PAD, levels), jnp.float32)
            flow[:, :, 1:1 + rows, strip] = jnp.zeros((STEPS, 4, rows, PAD, levels), jnp.float32)

    own_field.wait()
    receive(frac_copy, range(4))

    def arrive(s, f, r):
        @pl.when(t == r)
        def _():
            own_copy(s, f).wait()

        relayed = ((t == n - 2) & (r == 0)) | ((t == 1) & (r == n - 1))

        @pl.when((t != r) & jnp.logical_not(relayed))
        def _():
            forward_copy(s, f, r, t).wait_recv()

    def relay(s, f):
        for here, target, sources in relays:
            @pl.when(here)
            def _(target=target, sources=sources):
                for slot, r in enumerate(sources):
                    forward_copy(s, f, r, t).wait_recv()
                    forward_copy(s, f, r, target, slot).start()

    def collect(s):
        for f in (K, V):
            relay(s, f)
        for f in (K, V):
            for r in (0, n - 1):
                arrive(s, f, r)
        on_sides(functools.partial(flow_copy, s), (0, 1), "start")
        for f in (U, W):
            relay(s, f)
        for f, those in ((K, (1, 2)), (V, (1, 2)), (U, (1, 2, 0, 3))):
            for r in those:
                arrive(s, f, r)
        on_sides(functools.partial(flow_copy, s), (2, 3), "start")
        for r in range(n):
            arrive(s, W, r)
        receive(functools.partial(field_copy, s), range(4))
        receive(functools.partial(flow_copy, s), range(4))

    last_level = lax.broadcasted_iota(jnp.int32, (CHUNK, levels), 1) == levels - 1

    def advance(s, src, write):
        @pl.loop(0, rows + 1)
        def _(i):
            for c in range(0, cols, CHUNK):
                at = pl.ds(PAD + c, CHUNK)
                terms = face_terms(
                    flow[s, V, i, at], flow[s, V, i + 1, at],
                    flow[s, K, i, at], flow[s, K, i + 1, at], frac[i, at], frac[i + 1, at],
                )
                for a in range(tracer_count):
                    rflux[a, i, pl.ds(c, CHUNK)] = limited_flux(
                        src[a, i, at], src[a, i + 1, at], src[a, i + 2, at], src[a, i + 3, at],
                        *terms,
                    )

        @pl.loop(0, rows)
        def _(r):
            for c, size in [(c, CHUNK) for c in range(0, cols, CHUNK)] + [(cols - 7, 8)]:
                p, q = pl.ds(PAD + c - 1, size), pl.ds(PAD + c, size)
                terms = face_terms(
                    flow[s, U, r + 1, p], flow[s, U, r + 1, q],
                    flow[s, K, r + 1, p], flow[s, K, r + 1, q], frac[r + 1, p], frac[r + 1, q],
                )
                for a in range(tracer_count):
                    xflux[a, pl.ds(c, size)] = limited_flux(
                        src[a, r + 2, pl.ds(PAD + c - 2, size)], src[a, r + 2, p],
                        src[a, r + 2, q], src[a, r + 2, pl.ds(PAD + c + 1, size)], *terms,
                    )
            for c in range(0, cols, CHUNK):
                at = pl.ds(PAD + c, CHUNK)
                share = frac[r + 1, at]
                rise = flow[s, W, r + 1, at]
                area = jnp.where(
                    last_level, 0.0, jnp.minimum(share, pltpu.roll(share, levels - 1, 1))
                )
                lifted = area * rise
                upward = rise >= 0.0
                inverse = 1.0 / jnp.maximum(share, fraction_floor)
                for a in range(tracer_count):
                    centre = src[a, r + 2, at]
                    vertical = lifted * jnp.where(
                        upward, centre, pltpu.roll(centre, levels - 1, 1)
                    )
                    net = (
                        (rflux[a, r + 1, pl.ds(c, CHUNK)] - rflux[a, r, pl.ds(c, CHUNK)])
                        + (xflux[a, pl.ds(c + 1, CHUNK)] - xflux[a, pl.ds(c, CHUNK)])
                        + (vertical - pltpu.roll(vertical, 1, 1))
                    )
                    write(a, r, c, centre - net * inverse)

    def write_middle(a, r, c, value):
        c1[a, r + 2, pl.ds(PAD + c, CHUNK)] = value

    def write_out(a, r, c, value):
        out_ref[a, r, pl.ds(c, CHUNK)] = value

    collect(0)
    advance(0, c0, write_middle)
    on_sides(functools.partial(field_copy, 1), range(4), "start")
    collect(1)
    advance(1, c1, write_out)

    for s in range(STEPS):
        for f in range(4):
            for i in range(len(shifts)):
                @pl.when(groups[i][0])
                def _(s=s, f=f, i=i):
                    group_copy(s, f, i).wait_send()

            @pl.when((t == 1) | (t == n - 2))
            def _(s=s, f=f):
                for slot in range(1):
                    forward_copy(s, f, 0, t, slot).wait_send()
        on_sides(functools.partial(field_copy, s), range(4), "wait_send")
        on_sides(functools.partial(flow_copy, s), range(4), "wait_send")
    on_sides(frac_copy, range(4), "wait_send")


def fused_body(counts, tracers, land_mask, bottom_level, bottom_part, velocity, upwelling,
               diffusivity):
    tracer_count, rows, cols, levels = tracers.shape
    wide = cols + 2 * PAD
    row = (cols, levels)
    dma = pltpu.SemaphoreType.DMA
    hbm, vmem = pl.BlockSpec(memory_space=pltpu.HBM), pl.BlockSpec(memory_space=pltpu.VMEM)
    return pl.pallas_call(
        functools.partial(transport_kernel, counts),
        out_shape=jax.ShapeDtypeStruct(tracers.shape, jnp.float32),
        in_specs=[hbm] * 7,
        out_specs=vmem,
        scratch_shapes=[
            pltpu.VMEM((tracer_count, rows + 4, wide, levels), jnp.float32),
            pltpu.VMEM((tracer_count, rows + 4, wide, levels), jnp.float32),
            pltpu.VMEM((STEPS, 4, rows + 2, wide, levels), jnp.float32),
            pltpu.VMEM((rows + 2, wide, levels), jnp.float32),
            pltpu.VMEM((tracer_count, rows + 1, cols, levels), jnp.float32),
            pltpu.VMEM((tracer_count, cols + 8, levels), jnp.float32),
            pltpu.VMEM((rows, cols), jnp.int32),
            pltpu.VMEM((rows, cols), jnp.int32),
            pltpu.VMEM((rows, cols), jnp.float32),
            dma((STEPS, 4)), dma, dma((3,)),
            dma((STEPS, 4, 4)), dma((STEPS, 4, counts[0])), dma((STEPS, 4, 2)),
            dma((STEPS, 4)), dma((STEPS, 4)),
            dma((STEPS, 4)), dma((STEPS, 4)),
            dma((4,)), dma((4,)),
        ],
        compiler_params=pltpu.CompilerParams(
            collective_id=0, has_side_effects=True, vmem_limit_bytes=60 * 1024 * 1024
        ),
    )(
        tracers,
        velocity.reshape((STEPS, 2) + row),
        upwelling.reshape((STEPS,) + row),
        diffusivity.reshape((STEPS,) + row),
        land_mask, bottom_level, bottom_part,
    )


def solution(mesh):
    placed = (
        P("trc", "lat", "lon", None),
        P("lat", "lon"),
        P("lat", "lon"),
        P("lat", "lon"),
        P(None, None, ("lat", "lon"), "trc"),
        P(None, ("lat", "lon"), "trc"),
        P(None, ("lat", "lon"), "trc"),
    )
    counts = tuple(mesh.shape[axis] for axis in ("trc", "lat", "lon"))

    def body(*arrays):
        tracers, velocity = arrays[0], arrays[4]
        one_row = velocity.shape[3] == tracers.shape[2] * tracers.shape[3]
        if counts[0] == 4 and tracers.shape[1] == 4 and one_row:
            return fused_body(counts, *arrays)
        return gathered_body(*arrays)

    return jax.shard_map(
        body, mesh=mesh, in_specs=placed, out_specs=P("trc", "lat", "lon", None), check_vma=False
    )
```

```python
import functools

import jax
import jax.numpy as jnp
from jax import lax
from jax.experimental import pallas as pl
from jax.experimental.pallas import tpu as pltpu
from jax.sharding import PartitionSpec as P

STEPS = 2
MESH = pl.DeviceIdType.MESH


fraction_floor = 0.25


def with_halo(block, sides, width):
    for axis, dim in sides:
        count = lax.axis_size(axis)
        forward = [(i, i + 1) for i in range(count - 1)]
        backward = [(target, source) for source, target in forward]
        low = lax.ppermute(
            lax.slice_in_dim(block, block.shape[dim] - width, None, axis=dim), axis, forward
        )
        high = lax.ppermute(lax.slice_in_dim(block, 0, width, axis=dim), axis, backward)
        block = jnp.concatenate([low, block, high], axis=dim)
    return block


def minmod(first, second):
    return 0.5 * (jnp.sign(first) + jnp.sign(second)) * jnp.minimum(jnp.abs(first), jnp.abs(second))


def window(array, start, stop, offset):
    return lax.slice_in_dim(array, start, stop, axis=array.ndim + offset)


def face_divergence(field, speed, mixing, fraction, offset):
    extent = field.shape[field.ndim + offset]
    before = window(field, 0, extent - 3, offset)
    lower = window(field, 1, extent - 2, offset)
    upper = window(field, 2, extent - 1, offset)
    after = window(field, 3, extent, offset)
    face_speed = 0.5 * (window(speed, 1, extent - 2, offset) + window(speed, 2, extent - 1, offset))
    face_area = jnp.minimum(
        window(fraction, 1, extent - 2, offset), window(fraction, 2, extent - 1, offset)
    )
    face_mixing = 0.5 * (
        window(mixing, 1, extent - 2, offset) + window(mixing, 2, extent - 1, offset)
    )
    jump = upper - lower
    damping = 0.5 * (1.0 - jnp.abs(face_speed))
    from_lower = lower + damping * minmod(lower - before, jump)
    from_upper = upper - damping * minmod(jump, after - upper)
    face_value = jnp.where(face_speed >= 0.0, from_lower, from_upper)
    face_flux = face_area * (face_speed * face_value - face_mixing * jump)
    return window(face_flux, 1, extent - 3, offset) - window(face_flux, 0, extent - 4, offset)


def substep(field, fraction, eastward, northward, mixing, rising):
    across_rows = face_divergence(field, northward, mixing, fraction, -3)[..., 2:-2, :]
    across_cols = face_divergence(field, eastward, mixing, fraction, -2)[..., 2:-2, :, :]
    centre = field[..., 2:-2, 2:-2, :]
    wet_share = fraction[2:-2, 2:-2, :]
    top_area = jnp.minimum(wet_share[:, :, :-1], wet_share[:, :, 1:])
    lifting = rising[:, :, :-1]
    carried = jnp.where(lifting >= 0.0, centre[..., :-1], centre[..., 1:])
    vertical = top_area * lifting * carried
    closed = jnp.zeros(vertical.shape[:-1] + (1,), jnp.float32)
    across_levels = jnp.concatenate([vertical, closed], axis=-1) - jnp.concatenate(
        [closed, vertical], axis=-1
    )
    return centre - (across_rows + across_cols + across_levels) / jnp.maximum(
        wet_share, fraction_floor
    )


def cell_fraction(land_mask, bottom_level, bottom_part, levels):
    level_index = lax.broadcasted_iota(jnp.int32, land_mask.shape + (levels,), 2)
    deepest = bottom_level[:, :, None] - 1
    full_cell = (level_index < deepest).astype(jnp.float32)
    last_cell = (level_index == deepest).astype(jnp.float32) * bottom_part[:, :, None]
    return land_mask.astype(jnp.float32)[:, :, None] * (full_cell + last_cell)


def gathered_body(tracers, land_mask, bottom_level, bottom_part, velocity, upwelling, diffusivity):
    levels = tracers.shape[3]
    block_shape = (tracers.shape[1], tracers.shape[2], levels)
    fraction = cell_fraction(land_mask, bottom_level, bottom_part, levels)
    tracer_count = tracers.shape[0]
    moved = (
        lax.all_gather(velocity, "trc", axis=3, tiled=True),
        lax.all_gather(upwelling, "trc", axis=2, tiled=True),
        lax.all_gather(diffusivity, "trc", axis=2, tiled=True),
    )
    speeds = moved[0].reshape((STEPS, 2) + block_shape)
    rises = moved[1].reshape((STEPS,) + block_shape)
    mixes = moved[2].reshape((STEPS,) + block_shape)
    field = tracers
    wide_frac = fraction
    for number in range(STEPS):
        extras = [fraction[None]] if number == 0 else []
        stack = jnp.concatenate(
            [field] + extras + [jnp.stack([speeds[number, 0], speeds[number, 1], mixes[number]])],
            axis=0,
        )
        widened = with_halo(stack, (("lat", 1), ("lon", 2)), 2)
        if number == 0:
            wide_frac = widened[tracer_count]
        flows = widened[-3:]
        field = substep(
            widened[:tracer_count], wide_frac, flows[0], flows[1], flows[2], rises[number]
        )
    return field


U, K, V, W = range(4)
PAD = 8
CHUNK = 16


def limited_flux(before, lower, upper, after, east, scale, area_speed, area_mix):
    jump = upper - lower
    base = jnp.where(east, lower, upper)
    slope = jnp.where(east, lower - before, after - upper)
    limited = jnp.maximum(jnp.minimum(slope, jump), 0.0) + jnp.minimum(
        jnp.maximum(slope, jump), 0.0
    )
    return area_speed * (base + scale * limited) - area_mix * jump


def face_terms(speed_p, speed_q, mix_p, mix_q, frac_p, frac_q):
    speed = 0.5 * (speed_p + speed_q)
    area = jnp.minimum(frac_p, frac_q)
    east = speed >= 0.0
    damping = 0.5 * (1.0 - jnp.abs(speed))
    return east, jnp.where(east, damping, -damping), area * speed, area * (0.5 * (mix_p + mix_q))


def transport_kernel(
    counts, tr_hbm, vel_hbm, up_hbm, dif_hbm, mask_hbm, level_hbm, part_hbm, out_ref,
    c0, c1, flow, frac, rflux, xflux, mask_ref, level_ref, part_ref,
    own_sem, in_sem, column_sem, zs, zr, fs, cs, cr, fls, flr, frs, frr,
):
    n, n_lat, n_lon = counts
    tracer_count, rows, cols, levels = tr_hbm.shape
    t, la, lo = lax.axis_index("trc"), lax.axis_index("lat"), lax.axis_index("lon")
    inner = pl.ds(PAD, cols)
    left_halo, right_halo = pl.ds(0, PAD), pl.ds(PAD + cols, PAD)
    left_edge, right_edge = pl.ds(PAD, PAD), pl.ds(cols, PAD)

    sides = (
        (la > 0, {"lat": la - 1}),
        (la < n_lat - 1, {"lat": la + 1}),
        (lo > 0, {"lon": lo - 1}),
        (lo < n_lon - 1, {"lon": lo + 1}),
    )
    shifts = (2, -2, 1, -1)
    groups = (
        (t < n - 2, {"trc": t + 2}), (t >= 2, {"trc": t - 2}),
        (t < n - 1, {"trc": t + 1}), (t > 0, {"trc": t - 1}),
    )
    relays = ((t == n - 2, n - 1, (0,)), (t == 1, 0, (n - 1,)))

    columns = [
        pltpu.make_async_copy(src, dst, column_sem.at[i])
        for i, (src, dst) in enumerate(
            ((mask_hbm, mask_ref), (level_hbm, level_ref), (part_hbm, part_ref)))
    ]
    for copy in columns:
        copy.start()
    barrier = pltpu.get_barrier_semaphore()
    partners = sides + groups
    for there, device in partners:
        @pl.when(there)
        def _(device=device):
            pl.semaphore_signal(barrier, inc=1, device_id=device, device_id_type=MESH)

    def source(s, f):
        return {
            U: lambda: vel_hbm.at[s, 0], V: lambda: vel_hbm.at[s, 1],
            K: lambda: dif_hbm.at[s], W: lambda: up_hbm.at[s],
        }[f]()

    def group_copy(s, f, i):
        return pltpu.make_async_remote_copy(
            src_ref=source(s, f), dst_ref=flow.at[s, f, 1 + t, inner],
            send_sem=zs.at[s, f, i], recv_sem=zr.at[s, f, t],
            device_id=groups[i][1], device_id_type=MESH,
        )

    def forward_copy(s, f, r, target, slot=0):
        return pltpu.make_async_remote_copy(
            src_ref=flow.at[s, f, 1 + r, inner], dst_ref=flow.at[s, f, 1 + r, inner],
            send_sem=fs.at[s, f, slot], recv_sem=zr.at[s, f, r],
            device_id={"trc": target}, device_id_type=MESH,
        )

    def own_copy(s, f):
        return pltpu.make_async_copy(
            source(s, f), flow.at[s, f, 1 + t, inner], own_sem.at[s, f]
        )

    def side_copy(src, dst, send, recv, i):
        return pltpu.make_async_remote_copy(
            src_ref=src, dst_ref=dst, send_sem=send.at[i], recv_sem=recv.at[i],
            device_id=sides[i][1], device_id_type=MESH,
        )

    def field_copy(s, i):
        dst = c0 if s == 0 else c1
        if s == 0:
            srcs = (
                tr_hbm.at[:, pl.ds(0, 2)], tr_hbm.at[:, pl.ds(rows - 2, 2)],
                tr_hbm.at[:, :, pl.ds(0, PAD)], tr_hbm.at[:, :, pl.ds(cols - PAD, PAD)],
            )
        else:
            srcs = (
                c1.at[:, pl.ds(2, 2), inner], c1.at[:, pl.ds(rows, 2), inner],
                c1.at[:, pl.ds(2, rows), left_edge], c1.at[:, pl.ds(2, rows), right_edge],
            )
        dsts = (
            dst.at[:, pl.ds(rows + 2, 2), inner], dst.at[:, pl.ds(0, 2), inner],
            dst.at[:, pl.ds(2, rows), right_halo], dst.at[:, pl.ds(2, rows), left_halo],
        )
        return side_copy(srcs[i], dsts[i], cs.at[s], cr.at[s], i)

    def frac_copy(i):
        body = pl.ds(1, rows)
        srcs = (frac.at[1, inner], frac.at[rows, inner],
                frac.at[body, left_edge], frac.at[body, right_edge])
        dsts = (frac.at[rows + 1, inner], frac.at[0, inner],
                frac.at[body, right_halo], frac.at[body, left_halo])
        return side_copy(srcs[i], dsts[i], frs, frr, i)

    def flow_copy(s, i):
        body = pl.ds(1, rows)
        kv, uk = pl.ds(K, 2), pl.ds(U, 2)
        srcs = (flow.at[s, kv, 1, inner], flow.at[s, kv, rows, inner],
                flow.at[s, uk, body, left_edge], flow.at[s, uk, body, right_edge])
        dsts = (flow.at[s, kv, rows + 1, inner], flow.at[s, kv, 0, inner],
                flow.at[s, uk, body, right_halo], flow.at[s, uk, body, left_halo])
        return side_copy(srcs[i], dsts[i], fls.at[s], flr.at[s], i)

    opposite = (1, 0, 3, 2)

    def on_sides(make, which, act):
        for i in which:
            @pl.when(sides[i][0])
            def _(i=i):
                getattr(make(i), act)()

    def receive(make, which):
        for i in which:
            @pl.when(sides[opposite[i]][0])
            def _(i=i):
                make(i).wait_recv()

    def send_rows(s, fields, slots, when=None):
        for f in fields:
            for i in slots:
                @pl.when(groups[i][0] if when is None else groups[i][0] & when)
                def _(f=f, i=i):
                    group_copy(s, f, i).start()

    far, near = (0, 1), (2, 3)
    ends = (t == 0) | (t == n - 1)
    middle = jnp.logical_not(ends)
    own_field = pltpu.make_async_copy(tr_hbm, c0.at[:, pl.ds(2, rows), inner], in_sem)
    own_field.start()
    for f in (K, V, U, W):
        own_copy(0, f).start()
    for f in (K, V, U, W):
        own_copy(1, f).start()

    square = (cols, cols)
    eye = lax.broadcasted_iota(jnp.int32, square, 0) == lax.broadcasted_iota(jnp.int32, square, 1)
    level = lax.broadcasted_iota(jnp.int32, (cols, levels), 1).astype(jnp.float32)

    def upright(row):
        return jnp.sum(jnp.where(eye, jnp.broadcast_to(row, square), 0.0), axis=1, keepdims=True)

    for copy in columns:
        copy.wait()
    for r in range(rows):
        wet = mask_ref[r:r + 1, :].astype(jnp.float32)
        deepest = upright(level_ref[r:r + 1, :].astype(jnp.float32) - 1.0)
        share = upright(wet * part_ref[r:r + 1, :])
        wet = upright(wet)
        frac[1 + r, inner, :] = jnp.where(
            level < deepest, wet, jnp.where(level == deepest, share, 0.0)
        )

    @pl.when(la == 0)
    def _():
        for field in (c0, c1):
            field[:, 0:2] = jnp.zeros((tracer_count, 2) + field.shape[2:], jnp.float32)
        frac[0] = jnp.zeros(frac.shape[1:], jnp.float32)
        flow[:, :, 0] = jnp.zeros((STEPS, 4) + flow.shape[3:], jnp.float32)

    @pl.when(la == n_lat - 1)
    def _():
        for field in (c0, c1):
            field[:, rows + 2:] = jnp.zeros((tracer_count, 2) + field.shape[2:], jnp.float32)
        frac[rows + 1] = jnp.zeros(frac.shape[1:], jnp.float32)
        flow[:, :, rows + 1] = jnp.zeros((STEPS, 4) + flow.shape[3:], jnp.float32)

    for at_edge, strip in ((lo == 0, left_halo), (lo == n_lon - 1, right_halo)):
        @pl.when(at_edge)
        def _(strip=strip):
            for field in (c0, c1):
                field[:, 2:2 + rows, strip] = jnp.zeros(
                    (tracer_count, rows, PAD, levels), jnp.float32)
            frac[1:1 + rows, strip] = jnp.zeros((rows, PAD, levels), jnp.float32)
            flow[:, :, 1:1 + rows, strip] = jnp.zeros((STEPS, 4, rows, PAD, levels), jnp.float32)

    total = 0
    for there, _ in partners:
        total = total + jnp.where(there, 1, 0)
    pl.semaphore_wait(barrier, total)

    on_sides(frac_copy, range(4), "start")
    on_sides(functools.partial(field_copy, 0), range(4), "start")
    send_rows(0, (K, V), far + near)
    send_rows(1, (K, V), far + near, ends)
    send_rows(0, (U, W), far + near)
    send_rows(1, (K, V), near + far, middle)
    send_rows(1, (U, W), far + near)

    own_field.wait()
    receive(frac_copy, range(4))

    def arrive(s, f, r):
        @pl.when(t == r)
        def _():
            own_copy(s, f).wait()

        relayed = ((t == n - 2) & (r == 0)) | ((t == 1) & (r == n - 1))

        @pl.when((t != r) & jnp.logical_not(relayed))
        def _():
            forward_copy(s, f, r, t).wait_recv()

    def relay(s, f):
        for here, target, sources in relays:
            @pl.when(here)
            def _(target=target, sources=sources):
                for slot, r in enumerate(sources):
                    forward_copy(s, f, r, t).wait_recv()
                    forward_copy(s, f, r, target, slot).start()

    def edge_rows(s):
        for f in (K, V):
            for r in (0, n - 1):
                arrive(s, f, r)
        on_sides(functools.partial(flow_copy, s), (0, 1), "start")

    def mixed_columns(s):
        for f, those in ((K, (1, 2)), (V, (1, 2)), (U, (1, 2, 0, 3))):
            for r in those:
                arrive(s, f, r)
        on_sides(functools.partial(flow_copy, s), (2, 3), "start")
        for r in range(n):
            arrive(s, W, r)

    def collect_halos(s):
        receive(functools.partial(field_copy, s), range(4))
        receive(functools.partial(flow_copy, s), range(4))

    last_level = lax.broadcasted_iota(jnp.int32, (CHUNK, levels), 1) == levels - 1

    def advance(s, src, write):
        @pl.loop(0, rows + 1)
        def _(i):
            for c in range(0, cols, CHUNK):
                at = pl.ds(PAD + c, CHUNK)
                terms = face_terms(
                    flow[s, V, i, at], flow[s, V, i + 1, at],
                    flow[s, K, i, at], flow[s, K, i + 1, at], frac[i, at], frac[i + 1, at],
                )
                for a in range(tracer_count):
                    rflux[a, i, pl.ds(c, CHUNK)] = limited_flux(
                        src[a, i, at], src[a, i + 1, at], src[a, i + 2, at], src[a, i + 3, at],
                        *terms,
                    )

        @pl.loop(0, rows)
        def _(r):
            for c, size in [(c, CHUNK) for c in range(0, cols, CHUNK)] + [(cols - 7, 8)]:
                p, q = pl.ds(PAD + c - 1, size), pl.ds(PAD + c, size)
                terms = face_terms(
                    flow[s, U, r + 1, p], flow[s, U, r + 1, q],
                    flow[s, K, r + 1, p], flow[s, K, r + 1, q], frac[r + 1, p], frac[r + 1, q],
                )
                for a in range(tracer_count):
                    xflux[a, pl.ds(c, size)] = limited_flux(
                        src[a, r + 2, pl.ds(PAD + c - 2, size)], src[a, r + 2, p],
                        src[a, r + 2, q], src[a, r + 2, pl.ds(PAD + c + 1, size)], *terms,
                    )
            for c in range(0, cols, CHUNK):
                at = pl.ds(PAD + c, CHUNK)
                share = frac[r + 1, at]
                rise = flow[s, W, r + 1, at]
                area = jnp.where(
                    last_level, 0.0, jnp.minimum(share, pltpu.roll(share, levels - 1, 1))
                )
                lifted = area * rise
                upward = rise >= 0.0
                inverse = 1.0 / jnp.maximum(share, fraction_floor)
                for a in range(tracer_count):
                    centre = src[a, r + 2, at]
                    vertical = lifted * jnp.where(
                        upward, centre, pltpu.roll(centre, levels - 1, 1)
                    )
                    net = (
                        (rflux[a, r + 1, pl.ds(c, CHUNK)] - rflux[a, r, pl.ds(c, CHUNK)])
                        + (xflux[a, pl.ds(c + 1, CHUNK)] - xflux[a, pl.ds(c, CHUNK)])
                        + (vertical - pltpu.roll(vertical, 1, 1))
                    )
                    write(a, r, c, centre - net * inverse)

    def write_middle(a, r, c, value):
        c1[a, r + 2, pl.ds(PAD + c, CHUNK)] = value

    def write_out(a, r, c, value):
        out_ref[a, r, pl.ds(c, CHUNK)] = value

    for f in (K, V):
        relay(0, f)
    edge_rows(0)
    for f in (K, V):
        relay(1, f)
    relay(0, U)
    relay(0, W)
    edge_rows(1)
    mixed_columns(0)
    collect_halos(0)
    advance(0, c0, write_middle)
    on_sides(functools.partial(field_copy, 1), range(4), "start")
    for f in (U, W):
        relay(1, f)
    mixed_columns(1)
    collect_halos(1)
    advance(1, c1, write_out)

    for s in range(STEPS):
        for f in range(4):
            for i in range(len(shifts)):
                @pl.when(groups[i][0])
                def _(s=s, f=f, i=i):
                    group_copy(s, f, i).wait_send()

            @pl.when((t == 1) | (t == n - 2))
            def _(s=s, f=f):
                for slot in range(1):
                    forward_copy(s, f, 0, t, slot).wait_send()
        on_sides(functools.partial(field_copy, s), range(4), "wait_send")
        on_sides(functools.partial(flow_copy, s), range(4), "wait_send")
    on_sides(frac_copy, range(4), "wait_send")


def fused_body(counts, tracers, land_mask, bottom_level, bottom_part, velocity, upwelling,
               diffusivity):
    tracer_count, rows, cols, levels = tracers.shape
    wide = cols + 2 * PAD
    row = (cols, levels)
    dma = pltpu.SemaphoreType.DMA
    hbm, vmem = pl.BlockSpec(memory_space=pltpu.HBM), pl.BlockSpec(memory_space=pltpu.VMEM)
    return pl.pallas_call(
        functools.partial(transport_kernel, counts),
        out_shape=jax.ShapeDtypeStruct(tracers.shape, jnp.float32),
        in_specs=[hbm] * 7,
        out_specs=vmem,
        scratch_shapes=[
            pltpu.VMEM((tracer_count, rows + 4, wide, levels), jnp.float32),
            pltpu.VMEM((tracer_count, rows + 4, wide, levels), jnp.float32),
            pltpu.VMEM((STEPS, 4, rows + 2, wide, levels), jnp.float32),
            pltpu.VMEM((rows + 2, wide, levels), jnp.float32),
            pltpu.VMEM((tracer_count, rows + 1, cols, levels), jnp.float32),
            pltpu.VMEM((tracer_count, cols + 8, levels), jnp.float32),
            pltpu.VMEM((rows, cols), jnp.int32),
            pltpu.VMEM((rows, cols), jnp.int32),
            pltpu.VMEM((rows, cols), jnp.float32),
            dma((STEPS, 4)), dma, dma((3,)),
            dma((STEPS, 4, 4)), dma((STEPS, 4, counts[0])), dma((STEPS, 4, 2)),
            dma((STEPS, 4)), dma((STEPS, 4)),
            dma((STEPS, 4)), dma((STEPS, 4)),
            dma((4,)), dma((4,)),
        ],
        compiler_params=pltpu.CompilerParams(
            collective_id=0, has_side_effects=True, vmem_limit_bytes=60 * 1024 * 1024
        ),
    )(
        tracers,
        velocity.reshape((STEPS, 2) + row),
        upwelling.reshape((STEPS,) + row),
        diffusivity.reshape((STEPS,) + row),
        land_mask, bottom_level, bottom_part,
    )


def solution(mesh):
    placed = (
        P("trc", "lat", "lon", None),
        P("lat", "lon"),
        P("lat", "lon"),
        P("lat", "lon"),
        P(None, None, ("lat", "lon"), "trc"),
        P(None, ("lat", "lon"), "trc"),
        P(None, ("lat", "lon"), "trc"),
    )
    counts = tuple(mesh.shape[axis] for axis in ("trc", "lat", "lon"))

    def body(*arrays):
        tracers, velocity = arrays[0], arrays[4]
        one_row = velocity.shape[3] == tracers.shape[2] * tracers.shape[3]
        if counts[0] == 4 and tracers.shape[1] == 4 and one_row:
            return fused_body(counts, *arrays)
        return gathered_body(*arrays)

    return jax.shard_map(
        body, mesh=mesh, in_specs=placed, out_specs=P("trc", "lat", "lon", None), check_vma=False
    )
```

```python
import functools

import jax
import jax.numpy as jnp
from jax import lax
from jax.experimental import pallas as pl
from jax.experimental.pallas import tpu as pltpu
from jax.sharding import PartitionSpec as P

STEPS = 2
MESH = pl.DeviceIdType.MESH


fraction_floor = 0.25


def with_halo(block, sides, width):
    for axis, dim in sides:
        count = lax.axis_size(axis)
        forward = [(i, i + 1) for i in range(count - 1)]
        backward = [(target, source) for source, target in forward]
        low = lax.ppermute(
            lax.slice_in_dim(block, block.shape[dim] - width, None, axis=dim), axis, forward
        )
        high = lax.ppermute(lax.slice_in_dim(block, 0, width, axis=dim), axis, backward)
        block = jnp.concatenate([low, block, high], axis=dim)
    return block


def minmod(first, second):
    return 0.5 * (jnp.sign(first) + jnp.sign(second)) * jnp.minimum(jnp.abs(first), jnp.abs(second))


def window(array, start, stop, offset):
    return lax.slice_in_dim(array, start, stop, axis=array.ndim + offset)


def face_divergence(field, speed, mixing, fraction, offset):
    extent = field.shape[field.ndim + offset]
    before = window(field, 0, extent - 3, offset)
    lower = window(field, 1, extent - 2, offset)
    upper = window(field, 2, extent - 1, offset)
    after = window(field, 3, extent, offset)
    face_speed = 0.5 * (window(speed, 1, extent - 2, offset) + window(speed, 2, extent - 1, offset))
    face_area = jnp.minimum(
        window(fraction, 1, extent - 2, offset), window(fraction, 2, extent - 1, offset)
    )
    face_mixing = 0.5 * (
        window(mixing, 1, extent - 2, offset) + window(mixing, 2, extent - 1, offset)
    )
    jump = upper - lower
    damping = 0.5 * (1.0 - jnp.abs(face_speed))
    from_lower = lower + damping * minmod(lower - before, jump)
    from_upper = upper - damping * minmod(jump, after - upper)
    face_value = jnp.where(face_speed >= 0.0, from_lower, from_upper)
    face_flux = face_area * (face_speed * face_value - face_mixing * jump)
    return window(face_flux, 1, extent - 3, offset) - window(face_flux, 0, extent - 4, offset)


def substep(field, fraction, eastward, northward, mixing, rising):
    across_rows = face_divergence(field, northward, mixing, fraction, -3)[..., 2:-2, :]
    across_cols = face_divergence(field, eastward, mixing, fraction, -2)[..., 2:-2, :, :]
    centre = field[..., 2:-2, 2:-2, :]
    wet_share = fraction[2:-2, 2:-2, :]
    top_area = jnp.minimum(wet_share[:, :, :-1], wet_share[:, :, 1:])
    lifting = rising[:, :, :-1]
    carried = jnp.where(lifting >= 0.0, centre[..., :-1], centre[..., 1:])
    vertical = top_area * lifting * carried
    closed = jnp.zeros(vertical.shape[:-1] + (1,), jnp.float32)
    across_levels = jnp.concatenate([vertical, closed], axis=-1) - jnp.concatenate(
        [closed, vertical], axis=-1
    )
    return centre - (across_rows + across_cols + across_levels) / jnp.maximum(
        wet_share, fraction_floor
    )


def cell_fraction(land_mask, bottom_level, bottom_part, levels):
    level_index = lax.broadcasted_iota(jnp.int32, land_mask.shape + (levels,), 2)
    deepest = bottom_level[:, :, None] - 1
    full_cell = (level_index < deepest).astype(jnp.float32)
    last_cell = (level_index == deepest).astype(jnp.float32) * bottom_part[:, :, None]
    return land_mask.astype(jnp.float32)[:, :, None] * (full_cell + last_cell)


def gathered_body(tracers, land_mask, bottom_level, bottom_part, velocity, upwelling, diffusivity):
    levels = tracers.shape[3]
    block_shape = (tracers.shape[1], tracers.shape[2], levels)
    fraction = cell_fraction(land_mask, bottom_level, bottom_part, levels)
    tracer_count = tracers.shape[0]
    moved = (
        lax.all_gather(velocity, "trc", axis=3, tiled=True),
        lax.all_gather(upwelling, "trc", axis=2, tiled=True),
        lax.all_gather(diffusivity, "trc", axis=2, tiled=True),
    )
    speeds = moved[0].reshape((STEPS, 2) + block_shape)
    rises = moved[1].reshape((STEPS,) + block_shape)
    mixes = moved[2].reshape((STEPS,) + block_shape)
    field = tracers
    wide_frac = fraction
    for number in range(STEPS):
        extras = [fraction[None]] if number == 0 else []
        stack = jnp.concatenate(
            [field] + extras + [jnp.stack([speeds[number, 0], speeds[number, 1], mixes[number]])],
            axis=0,
        )
        widened = with_halo(stack, (("lat", 1), ("lon", 2)), 2)
        if number == 0:
            wide_frac = widened[tracer_count]
        flows = widened[-3:]
        field = substep(
            widened[:tracer_count], wide_frac, flows[0], flows[1], flows[2], rises[number]
        )
    return field


U, K, V, W = range(4)
PAD = 8
CHUNK = 16


def limited_flux(before, lower, upper, after, east, scale, area_speed, area_mix):
    jump = upper - lower
    base = jnp.where(east, lower, upper)
    slope = jnp.where(east, lower - before, after - upper)
    limited = jnp.maximum(jnp.minimum(slope, jump), 0.0) + jnp.minimum(
        jnp.maximum(slope, jump), 0.0
    )
    return area_speed * (base + scale * limited) - area_mix * jump


def face_terms(speed_p, speed_q, mix_p, mix_q, frac_p, frac_q):
    speed = 0.5 * (speed_p + speed_q)
    area = jnp.minimum(frac_p, frac_q)
    east = speed >= 0.0
    damping = 0.5 * (1.0 - jnp.abs(speed))
    return east, jnp.where(east, damping, -damping), area * speed, area * (0.5 * (mix_p + mix_q))


def transport_kernel(
    counts, tr_hbm, vel_hbm, up_hbm, dif_hbm, mask_hbm, level_hbm, part_hbm, out_ref,
    c0, c1, flow, frac, rflux, xflux, mask_ref, level_ref, part_ref,
    own_sem, in_sem, column_sem, zs, zr, fs, cs, cr, fls, flr, frs, frr,
):
    n, n_lat, n_lon = counts
    tracer_count, rows, cols, levels = tr_hbm.shape
    t, la, lo = lax.axis_index("trc"), lax.axis_index("lat"), lax.axis_index("lon")
    inner = pl.ds(PAD, cols)
    left_halo, right_halo = pl.ds(0, PAD), pl.ds(PAD + cols, PAD)
    left_edge, right_edge = pl.ds(PAD, PAD), pl.ds(cols, PAD)

    sides = (
        (la > 0, {"lat": la - 1}),
        (la < n_lat - 1, {"lat": la + 1}),
        (lo > 0, {"lon": lo - 1}),
        (lo < n_lon - 1, {"lon": lo + 1}),
    )
    shifts = (2, -2, 1, -1)
    groups = (
        (t < n - 2, {"trc": t + 2}), (t >= 2, {"trc": t - 2}),
        (t < n - 1, {"trc": t + 1}), (t > 0, {"trc": t - 1}),
    )
    relays = ((t == n - 2, n - 1, (0,)), (t == 1, 0, (n - 1,)))

    columns = [
        pltpu.make_async_copy(src, dst, column_sem.at[i])
        for i, (src, dst) in enumerate(
            ((mask_hbm, mask_ref), (level_hbm, level_ref), (part_hbm, part_ref)))
    ]
    for copy in columns:
        copy.start()
    barrier = pltpu.get_barrier_semaphore()
    partners = sides + groups
    for there, device in partners:
        @pl.when(there)
        def _(device=device):
            pl.semaphore_signal(barrier, inc=1, device_id=device, device_id_type=MESH)

    def source(s, f):
        return {
            U: lambda: vel_hbm.at[s, 0], V: lambda: vel_hbm.at[s, 1],
            K: lambda: dif_hbm.at[s], W: lambda: up_hbm.at[s],
        }[f]()

    def group_copy(s, f, i):
        return pltpu.make_async_remote_copy(
            src_ref=source(s, f), dst_ref=flow.at[s, f, 1 + t, inner],
            send_sem=zs.at[s, f, i], recv_sem=zr.at[s, f, t],
            device_id=groups[i][1], device_id_type=MESH,
        )

    def forward_copy(s, f, r, target, slot=0):
        return pltpu.make_async_remote_copy(
            src_ref=flow.at[s, f, 1 + r, inner], dst_ref=flow.at[s, f, 1 + r, inner],
            send_sem=fs.at[s, f, slot], recv_sem=zr.at[s, f, r],
            device_id={"trc": target}, device_id_type=MESH,
        )

    def own_copy(s, f):
        return pltpu.make_async_copy(
            source(s, f), flow.at[s, f, 1 + t, inner], own_sem.at[s, f]
        )

    def side_copy(src, dst, send, recv, i):
        return pltpu.make_async_remote_copy(
            src_ref=src, dst_ref=dst, send_sem=send.at[i], recv_sem=recv.at[i],
            device_id=sides[i][1], device_id_type=MESH,
        )

    def field_copy(s, i):
        dst = c0 if s == 0 else c1
        if s == 0:
            srcs = (
                tr_hbm.at[:, pl.ds(0, 2)], tr_hbm.at[:, pl.ds(rows - 2, 2)],
                tr_hbm.at[:, :, pl.ds(0, PAD)], tr_hbm.at[:, :, pl.ds(cols - PAD, PAD)],
            )
        else:
            srcs = (
                c1.at[:, pl.ds(2, 2), inner], c1.at[:, pl.ds(rows, 2), inner],
                c1.at[:, pl.ds(2, rows), left_edge], c1.at[:, pl.ds(2, rows), right_edge],
            )
        dsts = (
            dst.at[:, pl.ds(rows + 2, 2), inner], dst.at[:, pl.ds(0, 2), inner],
            dst.at[:, pl.ds(2, rows), right_halo], dst.at[:, pl.ds(2, rows), left_halo],
        )
        return side_copy(srcs[i], dsts[i], cs.at[s], cr.at[s], i)

    def frac_copy(i):
        body = pl.ds(1, rows)
        srcs = (frac.at[1, inner], frac.at[rows, inner],
                frac.at[body, left_edge], frac.at[body, right_edge])
        dsts = (frac.at[rows + 1, inner], frac.at[0, inner],
                frac.at[body, right_halo], frac.at[body, left_halo])
        return side_copy(srcs[i], dsts[i], frs, frr, i)

    def flow_copy(s, i):
        body = pl.ds(1, rows)
        kv, uk = pl.ds(K, 2), pl.ds(U, 2)
        srcs = (flow.at[s, kv, 1, inner], flow.at[s, kv, rows, inner],
                flow.at[s, uk, body, left_edge], flow.at[s, uk, body, right_edge])
        dsts = (flow.at[s, kv, rows + 1, inner], flow.at[s, kv, 0, inner],
                flow.at[s, uk, body, right_halo], flow.at[s, uk, body, left_halo])
        return side_copy(srcs[i], dsts[i], fls.at[s], flr.at[s], i)

    opposite = (1, 0, 3, 2)

    def on_sides(make, which, act):
        for i in which:
            @pl.when(sides[i][0])
            def _(i=i):
                getattr(make(i), act)()

    def receive(make, which):
        for i in which:
            @pl.when(sides[opposite[i]][0])
            def _(i=i):
                make(i).wait_recv()

    def send_rows(s, fields, slots, when=None):
        for f in fields:
            for i in slots:
                @pl.when(groups[i][0] if when is None else groups[i][0] & when)
                def _(f=f, i=i):
                    group_copy(s, f, i).start()

    far, near = (0, 1), (2, 3)
    ends = (t == 0) | (t == n - 1)
    middle = jnp.logical_not(ends)
    own_field = pltpu.make_async_copy(tr_hbm, c0.at[:, pl.ds(2, rows), inner], in_sem)
    own_field.start()
    for f in (K, V, U, W):
        own_copy(0, f).start()
    for f in (K, V, U, W):
        own_copy(1, f).start()

    square = (cols, cols)
    eye = lax.broadcasted_iota(jnp.int32, square, 0) == lax.broadcasted_iota(jnp.int32, square, 1)
    level = lax.broadcasted_iota(jnp.int32, (cols, levels), 1).astype(jnp.float32)

    def upright(row):
        return jnp.sum(jnp.where(eye, jnp.broadcast_to(row, square), 0.0), axis=1, keepdims=True)

    for copy in columns:
        copy.wait()
    for r in range(rows):
        wet = mask_ref[r:r + 1, :].astype(jnp.float32)
        deepest = upright(level_ref[r:r + 1, :].astype(jnp.float32) - 1.0)
        share = upright(wet * part_ref[r:r + 1, :])
        wet = upright(wet)
        frac[1 + r, inner, :] = jnp.where(
            level < deepest, wet, jnp.where(level == deepest, share, 0.0)
        )

    @pl.when(la == 0)
    def _():
        for field in (c0, c1):
            field[:, 0:2] = jnp.zeros((tracer_count, 2) + field.shape[2:], jnp.float32)
        frac[0] = jnp.zeros(frac.shape[1:], jnp.float32)
        flow[:, :, 0] = jnp.zeros((STEPS, 4) + flow.shape[3:], jnp.float32)

    @pl.when(la == n_lat - 1)
    def _():
        for field in (c0, c1):
            field[:, rows + 2:] = jnp.zeros((tracer_count, 2) + field.shape[2:], jnp.float32)
        frac[rows + 1] = jnp.zeros(frac.shape[1:], jnp.float32)
        flow[:, :, rows + 1] = jnp.zeros((STEPS, 4) + flow.shape[3:], jnp.float32)

    for at_edge, strip in ((lo == 0, left_halo), (lo == n_lon - 1, right_halo)):
        @pl.when(at_edge)
        def _(strip=strip):
            for field in (c0, c1):
                field[:, 2:2 + rows, strip] = jnp.zeros(
                    (tracer_count, rows, PAD, levels), jnp.float32)
            frac[1:1 + rows, strip] = jnp.zeros((rows, PAD, levels), jnp.float32)
            flow[:, :, 1:1 + rows, strip] = jnp.zeros((STEPS, 4, rows, PAD, levels), jnp.float32)

    total = 0
    for there, _ in partners:
        total = total + jnp.where(there, 1, 0)
    pl.semaphore_wait(barrier, total)

    on_sides(frac_copy, range(4), "start")
    on_sides(functools.partial(field_copy, 0), range(4), "start")
    send_rows(0, (K, V), far + near)
    send_rows(1, (K, V), far + near, ends)
    send_rows(0, (U, W), far + near)
    send_rows(1, (K, V), near + far, middle)
    send_rows(1, (U, W), far + near, ends)

    own_field.wait()
    receive(frac_copy, range(4))

    def arrive(s, f, r):
        @pl.when(t == r)
        def _():
            own_copy(s, f).wait()

        relayed = ((t == n - 2) & (r == 0)) | ((t == 1) & (r == n - 1))

        @pl.when((t != r) & jnp.logical_not(relayed))
        def _():
            forward_copy(s, f, r, t).wait_recv()

    def relay(s, f):
        for here, target, sources in relays:
            @pl.when(here)
            def _(target=target, sources=sources):
                for slot, r in enumerate(sources):
                    forward_copy(s, f, r, t).wait_recv()
                    forward_copy(s, f, r, target, slot).start()

    def edge_rows(s):
        for f in (K, V):
            for r in (0, n - 1):
                arrive(s, f, r)
        on_sides(functools.partial(flow_copy, s), (0, 1), "start")

    def mixed_columns(s):
        for f, those in ((K, (1, 2)), (V, (1, 2)), (U, (1, 2, 0, 3))):
            for r in those:
                arrive(s, f, r)
        on_sides(functools.partial(flow_copy, s), (2, 3), "start")
        for r in range(n):
            arrive(s, W, r)

    def collect_halos(s):
        receive(functools.partial(field_copy, s), range(4))
        receive(functools.partial(flow_copy, s), range(4))

    last_level = lax.broadcasted_iota(jnp.int32, (CHUNK, levels), 1) == levels - 1

    def advance(s, src, write):
        @pl.loop(0, rows + 1)
        def _(i):
            for c in range(0, cols, CHUNK):
                at = pl.ds(PAD + c, CHUNK)
                terms = face_terms(
                    flow[s, V, i, at], flow[s, V, i + 1, at],
                    flow[s, K, i, at], flow[s, K, i + 1, at], frac[i, at], frac[i + 1, at],
                )
                for a in range(tracer_count):
                    rflux[a, i, pl.ds(c, CHUNK)] = limited_flux(
                        src[a, i, at], src[a, i + 1, at], src[a, i + 2, at], src[a, i + 3, at],
                        *terms,
                    )

        @pl.loop(0, rows)
        def _(r):
            for c, size in [(c, CHUNK) for c in range(0, cols, CHUNK)] + [(cols - 7, 8)]:
                p, q = pl.ds(PAD + c - 1, size), pl.ds(PAD + c, size)
                terms = face_terms(
                    flow[s, U, r + 1, p], flow[s, U, r + 1, q],
                    flow[s, K, r + 1, p], flow[s, K, r + 1, q], frac[r + 1, p], frac[r + 1, q],
                )
                for a in range(tracer_count):
                    xflux[a, pl.ds(c, size)] = limited_flux(
                        src[a, r + 2, pl.ds(PAD + c - 2, size)], src[a, r + 2, p],
                        src[a, r + 2, q], src[a, r + 2, pl.ds(PAD + c + 1, size)], *terms,
                    )
            for c in range(0, cols, CHUNK):
                at = pl.ds(PAD + c, CHUNK)
                share = frac[r + 1, at]
                rise = flow[s, W, r + 1, at]
                area = jnp.where(
                    last_level, 0.0, jnp.minimum(share, pltpu.roll(share, levels - 1, 1))
                )
                lifted = area * rise
                upward = rise >= 0.0
                inverse = 1.0 / jnp.maximum(share, fraction_floor)
                for a in range(tracer_count):
                    centre = src[a, r + 2, at]
                    vertical = lifted * jnp.where(
                        upward, centre, pltpu.roll(centre, levels - 1, 1)
                    )
                    net = (
                        (rflux[a, r + 1, pl.ds(c, CHUNK)] - rflux[a, r, pl.ds(c, CHUNK)])
                        + (xflux[a, pl.ds(c + 1, CHUNK)] - xflux[a, pl.ds(c, CHUNK)])
                        + (vertical - pltpu.roll(vertical, 1, 1))
                    )
                    write(a, r, c, centre - net * inverse)

    def write_middle(a, r, c, value):
        c1[a, r + 2, pl.ds(PAD + c, CHUNK)] = value

    def write_out(a, r, c, value):
        out_ref[a, r, pl.ds(c, CHUNK)] = value

    for f in (K, V):
        relay(0, f)
    edge_rows(0)
    for f in (K, V):
        relay(1, f)
    relay(0, U)
    relay(0, W)
    edge_rows(1)
    mixed_columns(0)
    collect_halos(0)
    advance(0, c0, write_middle)
    send_rows(1, (U, W), far + near, middle)
    on_sides(functools.partial(field_copy, 1), range(4), "start")
    for f in (U, W):
        relay(1, f)
    mixed_columns(1)
    collect_halos(1)
    advance(1, c1, write_out)

    for s in range(STEPS):
        for f in range(4):
            for i in range(len(shifts)):
                @pl.when(groups[i][0])
                def _(s=s, f=f, i=i):
                    group_copy(s, f, i).wait_send()

            @pl.when((t == 1) | (t == n - 2))
            def _(s=s, f=f):
                for slot in range(1):
                    forward_copy(s, f, 0, t, slot).wait_send()
        on_sides(functools.partial(field_copy, s), range(4), "wait_send")
        on_sides(functools.partial(flow_copy, s), range(4), "wait_send")
    on_sides(frac_copy, range(4), "wait_send")


def fused_body(counts, tracers, land_mask, bottom_level, bottom_part, velocity, upwelling,
               diffusivity):
    tracer_count, rows, cols, levels = tracers.shape
    wide = cols + 2 * PAD
    row = (cols, levels)
    dma = pltpu.SemaphoreType.DMA
    hbm, vmem = pl.BlockSpec(memory_space=pltpu.HBM), pl.BlockSpec(memory_space=pltpu.VMEM)
    return pl.pallas_call(
        functools.partial(transport_kernel, counts),
        out_shape=jax.ShapeDtypeStruct(tracers.shape, jnp.float32),
        in_specs=[hbm] * 7,
        out_specs=vmem,
        scratch_shapes=[
            pltpu.VMEM((tracer_count, rows + 4, wide, levels), jnp.float32),
            pltpu.VMEM((tracer_count, rows + 4, wide, levels), jnp.float32),
            pltpu.VMEM((STEPS, 4, rows + 2, wide, levels), jnp.float32),
            pltpu.VMEM((rows + 2, wide, levels), jnp.float32),
            pltpu.VMEM((tracer_count, rows + 1, cols, levels), jnp.float32),
            pltpu.VMEM((tracer_count, cols + 8, levels), jnp.float32),
            pltpu.VMEM((rows, cols), jnp.int32),
            pltpu.VMEM((rows, cols), jnp.int32),
            pltpu.VMEM((rows, cols), jnp.float32),
            dma((STEPS, 4)), dma, dma((3,)),
            dma((STEPS, 4, 4)), dma((STEPS, 4, counts[0])), dma((STEPS, 4, 2)),
            dma((STEPS, 4)), dma((STEPS, 4)),
            dma((STEPS, 4)), dma((STEPS, 4)),
            dma((4,)), dma((4,)),
        ],
        compiler_params=pltpu.CompilerParams(
            collective_id=0, has_side_effects=True, vmem_limit_bytes=60 * 1024 * 1024
        ),
    )(
        tracers,
        velocity.reshape((STEPS, 2) + row),
        upwelling.reshape((STEPS,) + row),
        diffusivity.reshape((STEPS,) + row),
        land_mask, bottom_level, bottom_part,
    )


def solution(mesh):
    placed = (
        P("trc", "lat", "lon", None),
        P("lat", "lon"),
        P("lat", "lon"),
        P("lat", "lon"),
        P(None, None, ("lat", "lon"), "trc"),
        P(None, ("lat", "lon"), "trc"),
        P(None, ("lat", "lon"), "trc"),
    )
    counts = tuple(mesh.shape[axis] for axis in ("trc", "lat", "lon"))

    def body(*arrays):
        tracers, velocity = arrays[0], arrays[4]
        one_row = velocity.shape[3] == tracers.shape[2] * tracers.shape[3]
        if counts[0] == 4 and tracers.shape[1] == 4 and one_row:
            return fused_body(counts, *arrays)
        return gathered_body(*arrays)

    return jax.shard_map(
        body, mesh=mesh, in_specs=placed, out_specs=P("trc", "lat", "lon", None), check_vma=False
    )
```
